32 devices in a mesh: space: 8 (over y, x, core), level: 4 (over z).
Axes of the slice: x: 2, y: 2, z: 4, core: 2. Of those that a mesh axis runs over, the one named last changes fastest.
Arguments:
- fields: bfloat16 [4, 4096, 768], P('level', 'space'), may hold values from -16 to 16
- norm_vert: float32 [768], replicated, may hold values from 0.1 to 1.9
- query_vert: bfloat16 [768, 768], replicated, may hold values from -0.21875 to 0.21875
- keys_vert: bfloat16 [768, 768], replicated, may hold values from -0.21875 to 0.21875
- values_vert: bfloat16 [768, 768], replicated, may hold values from -0.21875 to 0.21875
- out_vert: bfloat16 [768, 768], replicated, may hold values from -0.21875 to 0.21875
- level_bias: float32 [12, 4, 4], replicated, may hold values from -3 to 250
- norm_patch: float32 [768], replicated, may hold values from 0.1 to 1.9
- query_patch: bfloat16 [768, 768], replicated, may hold values from -0.21875 to 0.21875
- keys_patch: bfloat16 [768, 768], replicated, may hold values from -0.21875 to 0.21875
- values_patch: bfloat16 [768, 768], replicated, may hold values from -0.21875 to 0.21875
- out_patch: bfloat16 [768, 768], replicated, may hold values from -0.21875 to 0.21875
- patch_bias: float32 [12, 2], replicated, may hold values from -3 to 250
- neighbours: int32 [16, 4], P('space'), may hold values from -1 to 15, as said below
- counts: int32 [16], P('space'), may hold values from 2 to 4, as said below
- cotangent: bfloat16 [4, 4096, 768], P('level', 'space'), may hold values from -0.046875 to 0.046875
Outputs:
- out_fields: bfloat16 [4, 4096, 768], P('level', 'space')
- grad_wo: float32 [768, 768], P('space')
The draws below stay inside these ranges and needn't reach their ends.
Inputs may be any that keep to these rules, and one draw needn't show every extreme that they name: `neighbours`: row p lists distinct patches, at most one from each device of space, held on devices at cycle distance 1 to 2 from the device of patch p (device s of space holds patches s * 2 to (s + 1) * 2 - 1); entries from counts[p] on are -1. `counts`: some patch has 4 neighbours in every draw.
All inputs are finite; a program needn't handle non-finite values.
Results may differ from the reference program's by a relative error of at most 0.025.
Values may be sent and summed in bfloat16 or wider, within the bound.
A program may use at most 128 MiB of HBM per device.

```python
import jax
import jax.numpy as jnp
from jax import lax

D = 768
H = 12
HD = 64
PATCH = 256
REACH = 2
PAT_DEV = 2
MAXN = 4
LEV = 4
PATCHES = 16
COLS = 4096
N_SPACE = 8


def draw_fields(key, part):
    noise_key = jax.random.fold_in(key, 0)
    sample = jax.random.normal(noise_key, (LEV, COLS, D), jnp.float32)
    return jnp.clip(sample, -16.0, 16.0).astype(jnp.bfloat16)


def draw_level_bias(key, part):
    noise_key = jax.random.fold_in(key, 0)
    sample = jnp.clip(jax.random.normal(noise_key, (H, LEV, LEV), jnp.float32), -3.0, 3.0)
    return sample


def draw_patch_bias(key, part):
    noise_key = jax.random.fold_in(jax.random.fold_in(key, 11), 0)
    sample = jnp.clip(jax.random.normal(noise_key, (H, 2), jnp.float32), -3.0, 3.0)
    return sample


def neighbour_tables(key):
    base_key = jax.random.fold_in(key, 29)
    order_key, count_key, within_key, full_key = jax.random.split(base_key, 4)
    orders = jax.vmap(lambda one_key: jax.random.permutation(one_key, 2 * REACH))(jax.random.split(order_key, PATCHES))
    signed = jnp.where(orders < REACH, orders + 1, REACH - 1 - orders)
    owners = jnp.arange(PATCHES, dtype=jnp.int32) // PAT_DEV
    far_owner = (owners[:, None] + signed) % N_SPACE
    within = jax.random.randint(within_key, (PATCHES, MAXN), 0, PAT_DEV)
    listed = far_owner * PAT_DEV + within
    tallies = jax.random.randint(count_key, (PATCHES,), 2, MAXN + 1)
    full_patch = jax.random.randint(full_key, (), 0, PATCHES)
    tallies = jnp.where(jnp.arange(PATCHES) == full_patch, MAXN, tallies)
    listed = jnp.where(jnp.arange(MAXN)[None, :] < tallies[:, None], listed, -1)
    return (listed.astype(jnp.int32), tallies.astype(jnp.int32))


def draw_neighbours(key, part):
    return neighbour_tables(key)[0]


def draw_counts(key, part):
    return neighbour_tables(key)[1]


def block_scale(key, dims, cuts, low, largest):
    level = 1.0
    for dim, blocks in cuts:
        steps = jax.random.uniform(jax.random.fold_in(jax.random.fold_in(key, 6), dim), (blocks,), jnp.float32, low / len(cuts), largest / len(cuts))
        level = level * jnp.repeat(jnp.exp(steps), dims[dim] // blocks).reshape((-1,) + (1,) * (len(dims) - 1 - dim))
    return level


def centred(own_key, dims, scale, bound, shards=(), kind=jnp.bfloat16):
    entries = jax.random.normal(own_key, dims, jnp.float32) * scale
    if len(shards) > 0:
        entries = block_scale(own_key, dims, shards, -0.22, 0.18) * entries
    return jnp.clip(entries, min=-bound, max=bound).astype(kind)


def setup_inputs(seed: int = 0) -> dict:
    streams_of = jax.random.split(jax.random.key(seed), 17)
    return {
        "fields": draw_fields(jax.random.fold_in(streams_of[16], 71), 0),
        "norm_vert": jnp.clip(1.0 + 0.18 * jax.random.normal(streams_of[1], (D,), jnp.float32), 0.1, 1.9),
        "query_vert": centred(streams_of[2], (D, D), D ** -0.5, 0.21875),
        "keys_vert": centred(streams_of[3], (D, D), D ** -0.5, 0.21875),
        "values_vert": centred(streams_of[4], (D, D), D ** -0.5, 0.21875),
        "out_vert": centred(streams_of[5], (D, D), D ** -0.5, 0.21875),
        "level_bias": draw_level_bias(jax.random.fold_in(streams_of[16], 71), 0),
        "norm_patch": jnp.clip(1.0 + 0.18 * jax.random.normal(streams_of[7], (D,), jnp.float32), 0.1, 1.9),
        "query_patch": centred(streams_of[8], (D, D), D ** -0.5, 0.21875),
        "keys_patch": centred(streams_of[9], (D, D), D ** -0.5, 0.21875),
        "values_patch": centred(streams_of[10], (D, D), D ** -0.5, 0.21875),
        "out_patch": centred(streams_of[11], (D, D), D ** -0.5, 0.21875),
        "patch_bias": draw_patch_bias(jax.random.fold_in(streams_of[16], 71), 0),
        "neighbours": draw_neighbours(jax.random.fold_in(streams_of[16], 71), 0),
        "counts": draw_counts(jax.random.fold_in(streams_of[16], 71), 0),
        "cotangent": centred(streams_of[15], (LEV, COLS, D), (LEV * COLS) ** -0.5, 0.046875, ((0, 4), (1, 8))),
    }


epsilon = 1e-06

def normalize(values, scaling):
    widened = values.astype(jnp.float32)
    mean_square = lax.optimization_barrier(jnp.mean(widened * widened, axis=-1, keepdims=True))
    return (widened * lax.rsqrt(mean_square + epsilon) * scaling).astype(jnp.bfloat16)

def project(inputs, weight):
    return jnp.dot(inputs, weight, preferred_element_type=jnp.float32).astype(jnp.bfloat16)

def vertical_mix(queries, keys_in, values_in, bias_table):
    level_count, columns, features = queries.shape
    query_heads = queries.astype(jnp.float32).reshape(level_count, columns, H, HD)
    key_heads = keys_in.astype(jnp.float32).reshape(keys_in.shape[0], columns, H, HD)
    value_heads = values_in.astype(jnp.float32).reshape(values_in.shape[0], columns, H, HD)
    scores = jnp.einsum('ichd,jchd->hijc', query_heads, key_heads) * HD ** (-0.5) + bias_table[:, :, :, None]
    weights = jax.nn.softmax(scores, axis=2).astype(jnp.bfloat16)
    mixture = jnp.einsum('hijc,jchd->ichd', weights.astype(jnp.float32), value_heads)
    return mixture.astype(jnp.bfloat16).reshape(level_count, columns, features)

def patch_mix(queries, own_keys, nearby, live_count, bias_table):
    features = queries.shape[-1]
    patch_len = own_keys.shape[0]
    keys_all = jnp.concatenate((own_keys[None], nearby), axis=0).reshape(-1, 2 * features)
    query_heads = queries.astype(jnp.float32).reshape(-1, H, HD)
    key_heads = keys_all[:, :features].astype(jnp.float32).reshape(-1, H, HD)
    value_heads = keys_all[:, features:].astype(jnp.float32).reshape(-1, H, HD)
    scores = jnp.einsum('qhd,khd->hqk', query_heads, key_heads) * HD ** (-0.5)
    block_bias = jnp.concatenate((bias_table[:, :1], jnp.broadcast_to(bias_table[:, 1:], (H, nearby.shape[0]))), axis=1)
    scores = scores + jnp.repeat(block_bias, patch_len, axis=1)[:, None, :]
    opened = jnp.repeat(jnp.arange(nearby.shape[0] + 1, dtype=jnp.int32) <= live_count, patch_len)
    scores = jnp.where(opened[None, None, :], scores, -jnp.inf)
    weights = jax.nn.softmax(scores, axis=-1).astype(jnp.bfloat16)
    mixture = jnp.einsum('hqk,khd->qhd', weights.astype(jnp.float32), value_heads)
    return mixture.astype(jnp.bfloat16).reshape(-1, features)

def reference(fields, norm_vert, query_vert, keys_vert, values_vert, out_vert, level_bias, norm_patch, query_patch, keys_patch, values_patch, out_patch, patch_bias, neighbours, counts, cotangent):
    normed = normalize(fields, norm_vert)
    attn_vert = vertical_mix(project(normed, query_vert), project(normed, keys_vert), project(normed, values_vert), level_bias)
    hidden = (fields.astype(jnp.float32) + jnp.dot(attn_vert, out_vert, preferred_element_type=jnp.float32)).astype(jnp.bfloat16)
    normed_patch = normalize(hidden, norm_patch)
    queries = project(normed_patch, query_patch).reshape(LEV, PATCHES, PATCH, D)
    key_values = jnp.concatenate((project(normed_patch, keys_patch), project(normed_patch, values_patch)), axis=-1).reshape(LEV, PATCHES, PATCH, 2 * D)

    def one_patch(patch_index):
        near_ids = jnp.maximum(neighbours[patch_index], 0).astype(jnp.int32)
        nearby = jnp.take(key_values, near_ids, axis=1)
        own_keys = key_values[:, patch_index]
        own_queries = queries[:, patch_index]
        return jax.vmap(patch_mix, in_axes=(0, 0, 0, None, None))(own_queries, own_keys, nearby, counts[patch_index], patch_bias)
    mixture = lax.map(one_patch, jnp.arange(PATCHES, dtype=jnp.int32))
    attn_patch = jnp.moveaxis(mixture, 0, 1).reshape(LEV, COLS, D)
    out_fields = (hidden.astype(jnp.float32) + jnp.dot(attn_patch, out_patch, preferred_element_type=jnp.float32)).astype(jnp.bfloat16)
    grad_wo = lax.dot_general(attn_patch.reshape(-1, D), cotangent.reshape(-1, D), (((0,), (0,)), ((), ())), preferred_element_type=jnp.float32)
    return (out_fields, grad_wo)
```

```python
import functools
import math

import jax
import jax.numpy as jnp
from jax import lax
from jax.experimental import pallas as pl
from jax.experimental.pallas import tpu as pltpu
from jax.sharding import PartitionSpec as P

HD = 64
PATCH = 256
LANES = 128
ROWS = 16
DEPTH = 3
VMEM_LIMIT = 58 * 1024 * 1024

epsilon = 1e-06


def normalized(widened, scaling):
    mean_square = jnp.mean(widened * widened, axis=-1, keepdims=True)
    return (widened * lax.rsqrt(mean_square + epsilon) * scaling).astype(jnp.bfloat16)


def project(inputs, weight):
    return jnp.dot(inputs, weight, preferred_element_type=jnp.float32).astype(jnp.bfloat16)


def vertical(x, gain, wq, wk, wv, wo, bias_rows, gather_heads, spread_heads):
    levels, columns, features = x.shape
    tokens = levels * columns
    x = x.reshape(tokens, features).astype(jnp.float32)
    normed = normalized(x, gain)
    queries = project(normed, wq).astype(jnp.float32)
    keys = project(normed, wk).astype(jnp.float32)
    values = project(normed, wv).astype(jnp.float32)
    part = lambda array, i: array[i * columns : (i + 1) * columns]
    products = jnp.concatenate(
        [(part(queries, i) * part(keys, j)).astype(jnp.bfloat16) for i in range(levels) for j in range(levels)], axis=0
    )
    summed = jnp.dot(products, gather_heads, preferred_element_type=jnp.float32) * HD ** (-0.5)
    weights = []
    for i in range(levels):
        scores = [part(summed, i * levels + j) + bias_rows[i * levels + j] for j in range(levels)]
        top = functools.reduce(jnp.maximum, scores)
        raised = [jnp.exp(score - top) for score in scores]
        inverse = 1.0 / functools.reduce(jnp.add, raised)
        weights += [(each * inverse).astype(jnp.bfloat16) for each in raised]
    spread = jnp.dot(jnp.concatenate(weights, axis=0), spread_heads, preferred_element_type=jnp.float32)
    mixed = [
        functools.reduce(jnp.add, [part(spread, i * levels + j) * part(values, j) for j in range(levels)])
        for i in range(levels)
    ]
    attn = jnp.concatenate(mixed, axis=0).astype(jnp.bfloat16)
    hidden = x + jnp.dot(attn, wo, preferred_element_type=jnp.float32)
    return hidden.astype(jnp.bfloat16).reshape(levels, columns, features)


def choices(nb_ref, count_ref, patch, source, per_device):
    live = jnp.int32(0)
    within = jnp.int32(0)
    for m in range(nb_ref.shape[1]):
        listed = jnp.maximum(nb_ref[patch, m], 0)
        hit = jnp.logical_and(m < count_ref[patch], lax.div(listed, per_device) == source)
        live = jnp.where(hit, 1, live)
        within = jnp.where(hit, lax.rem(listed, per_device), within)
    return live, within


def score(step, patch, parity, parts, q_ref, k_ref):
    low = lax.broadcasted_iota(jnp.int32, (1, LANES), 1) < HD
    mine = low if parity == 0 else jnp.logical_not(low)
    lanes = pl.ds(pl.multiple_of(step * LANES, LANES), LANES)
    query = q_ref[pl.ds(patch * PATCH, PATCH), lanes]
    query = jnp.where(mine, query, jnp.zeros_like(query))
    keys = jnp.concatenate([k_ref[block, pl.ds(first, count), lanes] for block, first, count, _ in parts], axis=0)
    return lax.dot_general(keys, query, (((1,), (1,)), ((), ())), preferred_element_type=jnp.float32)


def soften(scores, parts, before):
    pieces, at = [], 0
    for _, _, count, add in parts:
        pieces.append((scores[at : at + count], add))
        at += count
    top = functools.reduce(jnp.maximum, [jnp.max(s, axis=0, keepdims=True) + a for s, a in pieces])
    if before is not None:
        top = jnp.maximum(top, before)
    raised = [jnp.exp2(s + (a - top)) for s, a in pieces]
    total = functools.reduce(jnp.add, [jnp.sum(r, axis=0, keepdims=True) for r in raised])
    return top, total, jnp.concatenate([r.astype(jnp.bfloat16) for r in raised], axis=0)


def mix(step, parity, raised, parts, vt_ref):
    rows = pl.ds(pl.multiple_of(step * LANES + parity * HD, HD), HD)
    values = jnp.concatenate([vt_ref[block, rows, pl.ds(first, count)] for block, first, count, _ in parts], axis=1)
    return jnp.dot(values, raised, preferred_element_type=jnp.float32)


def attend(step, patches, second, parts_of, q_ref, k_ref, vt_ref, top_ref, finish):
    heads = [(patch, parity) for patch in range(patches) for parity in range(2)]
    parts = [parts_of(patch, step * 2 + parity, second) for patch, parity in heads]
    slots = [patch * top_ref.shape[0] // patches + step * 2 + parity for patch, parity in heads]
    befores = [top_ref[slot] if second else None for slot in slots]
    scores, soft = {}, {}
    for turn in range(len(heads) + 2):
        if turn < len(heads):
            patch, parity = heads[turn]
            scores[turn] = score(step, patch, parity, parts[turn], q_ref, k_ref)
        if 1 <= turn < len(heads) + 1:
            soft[turn - 1] = soften(scores.pop(turn - 1), parts[turn - 1], befores[turn - 1])
        if turn >= 2:
            at = turn - 2
            top, total, raised = soft.pop(at)
            finish(slots[at], *heads[at], befores[at], top, total, mix(step, heads[at][1], raised, parts[at], vt_ref))


def remote(src, dst, send, recv, device):
    return pltpu.make_async_remote_copy(
        src_ref=src, dst_ref=dst, send_sem=send, recv_sem=recv, device_id=device,
        device_id_type=pl.DeviceIdType.MESH,
    )


def whole_kernel(cycle, levels, x_ref, nv_ref, np_ref, wqv_hbm, wkv_hbm, wvv_hbm, wov_hbm, wqp_hbm, wkp_hbm, wvp_hbm,
                 wop_hbm, cot_hbm, lb_ref, pb_ref, nb_ref, count_ref, out_ref, grad_ref, weight_ref, wvt_ref, gather_ref,
                 spread_ref, cot_ref, in_ref, hsend_ref, hid_ref, own_ref, far_ref, q_ref, k_ref, vt_ref, attn_ref,
                 gsend_ref, gpair_ref, gsum_ref, grecv_ref, lsend_ref, lrecv_ref, final_ref, top_ref, total_ref, mixed_ref, load_sem, in_send,
                 in_recv, back_send, back_recv, halo_send, halo_recv, pair_send, pair_recv, share_send, share_recv, part_send, part_recv,
                 full_send, full_recv):
    chunks, _, columns, features = x_ref.shape
    size = levels * columns
    split = PATCH // size
    patches = chunks // split
    half = max(LANES, size)
    group = half // size
    order = [patch * split + turn for turn in range(split) for patch in range(patches)]
    place = lax.axis_index("space")
    level = lax.axis_index("level")
    weights_hbm = (wqv_hbm, wkv_hbm, wvv_hbm, wov_hbm, wqp_hbm, wkp_hbm, wvp_hbm, wop_hbm)
    loads = [pltpu.make_async_copy(w, weight_ref.at[i], load_sem.at[i]) for i, w in enumerate(weights_hbm)]
    loads.append(pltpu.make_async_copy(cot_hbm, cot_ref, load_sem.at[len(weights_hbm)]))
    for load in loads:
        load.start()

    barrier = pltpu.get_barrier_semaphore()
    peers = [lax.rem(level + k, levels) for k in range(1, levels)]
    around = [lax.rem(place + k, cycle) for k in range(1, cycle)]
    for peer in peers:
        pl.semaphore_signal(barrier, inc=1, device_id={"level": peer}, device_id_type=pl.DeviceIdType.MESH)
    for peer in around:
        pl.semaphore_signal(barrier, inc=1, device_id={"space": peer}, device_id_type=pl.DeviceIdType.MESH)
    pl.semaphore_wait(barrier, levels - 1 + cycle - 1)

    inward, back, sent = [], [], []

    def send_in(i):
        c = order[i]
        steps = []
        for k, peer in enumerate(peers):
            steps.append(remote(x_ref.at[c, peer], in_ref.at[c, level], in_send.at[c, k], in_recv.at[c, k],
                                {"level": peer}))
            steps[-1].start()
        in_ref[c, level] = x_ref[c, level]
        inward.append(steps)

    for i in range(min(DEPTH, chunks)):
        send_in(i)

    lane = lax.broadcasted_iota(jnp.int32, (1, LANES), 1)
    bias_rows = []
    for i in range(levels):
        for j in range(levels):
            row = jnp.zeros((1, LANES), jnp.float32)
            for h in range(lb_ref.shape[2]):
                row = jnp.where(lane == h, lb_ref[i, j, h], row)
            bias_rows.append(row)
    head_of = lax.broadcasted_iota(jnp.int32, (features, LANES), 0) // HD
    gather_ref[...] = (head_of == lax.broadcasted_iota(jnp.int32, (features, LANES), 1)).astype(jnp.bfloat16)
    head_to = lax.broadcasted_iota(jnp.int32, (LANES, features), 1) // HD
    spread_ref[...] = (head_to == lax.broadcasted_iota(jnp.int32, (LANES, features), 0)).astype(jnp.bfloat16)
    for load in loads[:4]:
        load.wait()

    def vertical_step(i):
        c = order[i]
        for step in inward[i]:
            step.wait_recv()
        hsend_ref[c] = vertical(in_ref[c], nv_ref[...][None], weight_ref[0], weight_ref[1], weight_ref[2],
                                weight_ref[3], bias_rows, gather_ref[...], spread_ref[...])
        steps = []
        for k, peer in enumerate(peers):
            steps.append(remote(hsend_ref.at[c, peer], hid_ref.at[c, level], back_send.at[c, k], back_recv.at[c, k],
                                {"level": peer}))
            steps[-1].start()
        hid_ref[c, level] = hsend_ref[c, level]
        back.append(steps)
        if i + DEPTH < chunks:
            send_in(i + DEPTH)
        if i == 0:
            for load in loads[4:]:
                load.wait()
            wvt_ref[...] = weight_ref[6].T

    chips = cycle // 2
    chip, core = lax.div(place, 2), lax.rem(place, 2)
    toward = core * 2 - 1
    sources = [lax.rem(place + step * toward + 2 * cycle, cycle) for step in (1, 2, -1, -2)]
    partner = sources[2]
    far = len(sources) * patches
    scale = HD ** (-0.5) * math.log2(math.e)
    relayed = chips == 4
    odd = lax.rem(chip + core, 2)
    near, diagonal = (3 - 2 * odd, 1 + 2 * odd) if relayed else (1, 3)
    beside = (chip + 1 - 2 * lax.rem(chip, 2)) * 2 + core
    across = lax.rem(chip + 2, chips) * 2 + core

    def halo_copy(c, src, slot, lane_of, device):
        return remote(src, far_ref.at[slot, c], halo_send.at[c, lane_of], halo_recv.at[c, slot], {"space": device})

    def begin(make):
        make().start()
        sent.append(make)

    def halo_step(i):
        c = order[i]
        for step in back[i]:
            step.wait_recv()
        own_ref[c] = normalized(hid_ref[c].reshape(size, features).astype(jnp.float32), np_ref[...][None])
        if relayed:
            begin(lambda: halo_copy(c, own_ref.at[c], diagonal, 0, beside))
        else:
            begin(lambda: halo_copy(c, own_ref.at[c], 3, 0, sources[1]))
            begin(lambda: halo_copy(c, own_ref.at[c], 1, 2, sources[3]))
        begin(lambda: halo_copy(c, own_ref.at[c], 2, 1, partner))

    def relay_step(i):
        c = order[i]
        halo_copy(c, own_ref.at[c], near, 0, beside).wait_recv()
        if relayed:
            begin(lambda: halo_copy(c, far_ref.at[near, c], diagonal, 2, across))

    def forward_step(i):
        c = order[i]
        halo_copy(c, own_ref.at[c], diagonal, 0, across).wait_recv()
        begin(lambda: halo_copy(c, far_ref.at[3, c], 0, 3, partner))

    def members(patch, part):
        return [patch * split + part * group + k for k in range(group)]

    def keys_values(normed, blocks, part):
        keys = project(normed, weight_ref[5])
        values = lax.dot_general(
            wvt_ref[...], normed, (((1,), (1,)), ((), ())), preferred_element_type=jnp.float32
        ).astype(jnp.bfloat16)
        for k, block in enumerate(blocks):
            k_ref[block, part * half : (part + 1) * half, :] = keys[k * half : (k + 1) * half]
            vt_ref[block, :, part * half : (part + 1) * half] = values[:, k * half : (k + 1) * half]

    def own_half(patch, part):
        first = members(patch, part)[0]
        normed = own_ref[first : first + group].reshape(half, features)
        queries = jnp.dot(normed, weight_ref[4], preferred_element_type=jnp.float32) * scale
        q_ref[first * size : first * size + half, :] = queries.astype(jnp.bfloat16)
        keys_values(normed, (far + patch,), part)

    def far_half(slots, patch, part):
        first = members(patch, part)[0]
        for slot in slots:
            if slot in (0, 2):
                for c in members(patch, part):
                    halo_copy(c, own_ref.at[c], slot, 1, partner).wait_recv()
        normed = jnp.concatenate([far_ref[slot, first : first + group].reshape(half, features) for slot in slots], axis=0)
        keys_values(normed, [slot * patches + patch for slot in slots], part)

    halves = PATCH // half
    arrival = [i + 2.4 if i < chunks - 2 else chunks - 0.6 + 0.5 * (i - chunks + 3) for i in range(chunks)]
    events = []
    for i in range(chunks):
        events.append((float(i), vertical_step, (i,)))
        events.append((arrival[i], halo_step, (i,)))
        events.append((arrival[i] + 0.9, relay_step, (i,)))
        events.append((arrival[i] + 1.8, forward_step, (i,)))
    for patch in range(patches):
        for part in range(halves):
            last = order.index(members(patch, part)[-1])
            events.append((arrival[last] + 0.05, own_half, (patch, part)))
            events.append((arrival[last] + 0.35, far_half, ((2,), patch, part)))
            events.append((arrival[last] + 2.2, far_half, ((1, 3, 0), patch, part)))
    events.sort(key=lambda event: event[0])
    start = arrival[-1] + 0.5
    pairs = features // LANES
    late = [event for event in events if event[0] > start]
    for _, act, args in events:
        if _ <= start:
            act(*args)
    tables = [[choices(nb_ref, count_ref, patch, source, patches) for source in sources] for patch in range(patches)]

    def parts_of(patch, head, second):
        log2e = jnp.float32(math.log2(math.e))
        adds = [jnp.where(live > 0, pb_ref[1, head], jnp.float32(-1e30)) * log2e for live, _ in tables[patch]]
        block = [slot * patches + tables[patch][slot][1] for slot in range(len(sources))]
        count = PATCH - half
        if second:
            return [(block[slot], count, half, adds[slot]) for slot in (0, 1, 3)]
        own = [(far + patch, 0, PATCH, pb_ref[0, head] * log2e), (block[2], 0, PATCH, adds[2])]
        return own + [(block[slot], 0, count, adds[slot]) for slot in (0, 1, 3)]

    inside = [event for event in late if event[1] in (relay_step, forward_step)][:2]
    after = [event for event in late if event not in inside]

    def early_pair(step, carry):
        for turn, (_, act, args) in zip((2, 4), inside):

            @pl.when(step == turn)
            def _():
                act(*args)

        def finish(slot, patch, parity, before, top, total, mixed):
            top_ref[slot] = top
            total_ref[slot] = total
            mixed_ref[slot] = mixed

        attend(step, patches, False, parts_of, q_ref, k_ref, vt_ref, top_ref, finish)
        return carry

    lax.fori_loop(0, pairs, early_pair, 0)
    for _, act, args in after:
        act(*args)

    share = features // cycle
    grain = gsend_ref.shape[1]
    per_pair = LANES // grain
    per_owner = share // grain

    def pair_copy(index):
        slot = lax.div(index, 2 * per_owner) * per_owner + lax.rem(index, per_owner)
        return slot, remote(gsend_ref.at[index], gpair_ref.at[slot], pair_send.at[slot], pair_recv.at[slot],
                            {"space": partner})

    def share_copy(slot):
        owner = lax.div(slot, per_owner)
        gap = lax.rem(chip - owner + chips, chips)
        there = jnp.maximum(gap - 1, 0) * per_owner + lax.rem(slot, per_owner)
        return owner, remote(gsum_ref.at[slot], grecv_ref.at[there], share_send.at[slot], share_recv.at[there],
                             {"space": owner * 2 + core})

    def gather_pair(step):
        for part in range(per_pair):
            index = step * per_pair + part

            @pl.when(lax.rem(lax.div(index, per_owner), 2) == core)
            def _():
                slot, copy = pair_copy(index)
                copy.wait_recv()
                both = gsend_ref[index].astype(jnp.float32) + gpair_ref[slot].astype(jnp.float32)
                gsum_ref[slot] = both.astype(jnp.bfloat16)
                owner, copy = share_copy(slot)

                @pl.when(owner != chip)
                def _():
                    copy.start()

    def step_of(turn):
        return lax.rem(lax.div(chip * pairs, chips) + 2 + turn, pairs)

    def pair(turn, carry):
        step = step_of(turn)

        def finish(slot, patch, parity, before, top, total, mixed):
            fade = jnp.exp2(before - top)
            mixed = (mixed + mixed_ref[slot] * fade) * (1.0 / (total + total_ref[slot] * fade))
            rows = pl.ds(pl.multiple_of(step * LANES + parity * HD, HD), HD)
            attn_ref[rows, patch * PATCH : (patch + 1) * PATCH] = mixed.astype(jnp.bfloat16)

        attend(step, patches, True, parts_of, q_ref, k_ref, vt_ref, top_ref, finish)
        rows = pl.ds(pl.multiple_of(step * LANES, LANES), LANES)
        total = jnp.dot(attn_ref[rows, :], cot_ref[...], preferred_element_type=jnp.float32).astype(jnp.bfloat16)
        for part in range(per_pair):
            gsend_ref[step * per_pair + part] = total[part * grain : (part + 1) * grain]
        for part in range(per_pair):
            index = step * per_pair + part

            @pl.when(lax.rem(lax.div(index, per_owner), 2) != core)
            def _():
                pair_copy(index)[1].start()

        @pl.when(turn > 0)
        def _():
            gather_pair(step_of(turn - 1))

        return carry

    lax.fori_loop(0, pairs, pair, 0)
    gather_pair(step_of(pairs - 1))
    mixture = lax.dot_general(
        attn_ref[...], weight_ref[7], (((0,), (0,)), ((), ())), preferred_element_type=jnp.float32
    )
    out_ref[...] = (hid_ref[...].reshape(patches * PATCH, features).astype(jnp.float32) + mixture).astype(jnp.bfloat16)
    sums = []
    for part in range(per_owner):
        sums.append(gsum_ref[chip * per_owner + part].astype(jnp.float32))
        for k in range(chips - 1):
            slot = k * per_owner + part
            remote(gsum_ref.at[0], grecv_ref.at[slot], share_send.at[0], share_recv.at[slot],
                   {"space": partner}).wait_recv()
            sums[-1] = sums[-1] + grecv_ref[slot].astype(jnp.float32)
    gathered = jnp.concatenate(sums, axis=0)
    piece = share // levels
    for i in range(levels):
        lsend_ref[i] = gathered[i * piece : (i + 1) * piece].astype(jnp.bfloat16)
    parts = []
    for k, peer in enumerate(peers):
        parts.append(remote(lsend_ref.at[peer], lrecv_ref.at[k], part_send.at[k], part_recv.at[k], {"level": peer}))
        parts[-1].start()
    gathered = lsend_ref[level].astype(jnp.float32)
    for k, step in enumerate(parts):
        step.wait_recv()
        gathered = gathered + lrecv_ref[k].astype(jnp.float32)
    final_ref[level] = gathered.astype(jnp.bfloat16)
    fulls = []
    for k, peer in enumerate(peers):
        fulls.append(remote(final_ref.at[level], final_ref.at[level], full_send.at[k], full_recv.at[k],
                            {"level": peer}))
        fulls[-1].start()
    for step in fulls:
        step.wait_recv()
    for i in range(levels):
        grad_ref[i * piece : (i + 1) * piece, :] = final_ref[i].astype(jnp.float32)
    for steps in inward + back + [[make() for make in sent], parts, fulls]:
        for step in steps:
            step.wait_send()

    def drained(slot, carry):
        index = lax.div(slot, per_owner) * 2 * per_owner + (1 - core) * per_owner + lax.rem(slot, per_owner)
        pair_copy(index)[1].wait_send()
        owner, copy = share_copy(slot)

        @pl.when(owner != chip)
        def _():
            copy.wait_send()

        return carry

    lax.fori_loop(0, chips * per_owner, drained, 0)


def body(fields, norm_vert, query_vert, keys_vert, values_vert, out_vert, level_bias, norm_patch, query_patch,
         keys_patch, values_patch, out_patch, patch_bias, neighbours, counts, cotangent):
    _, tokens, features = fields.shape
    levels = lax.axis_size("level")
    cycle = lax.axis_size("space")
    patches = tokens // PATCH
    columns = ROWS
    size = levels * columns
    chunks = tokens // size
    pairs = features // LANES
    grain = math.gcd(features // cycle, LANES)
    share = features // cycle
    x = fields.reshape(chunks, levels, columns, features)
    vmem = pl.BlockSpec(memory_space=pltpu.VMEM)
    smem = pl.BlockSpec(memory_space=pltpu.SMEM)
    hbm = pl.BlockSpec(memory_space=pl.ANY)
    narrow = lambda *shape: pltpu.VMEM(shape, jnp.bfloat16)
    dma = lambda *shape: pltpu.SemaphoreType.DMA(shape)
    blocks = 5 * patches
    out, grad = pl.pallas_call(
        functools.partial(whole_kernel, cycle, levels),
        out_shape=(
            jax.ShapeDtypeStruct((tokens, features), jnp.bfloat16),
            jax.ShapeDtypeStruct((share, features), jnp.float32),
        ),
        in_specs=[vmem] * 3 + [hbm] * 9 + [smem] * 4,
        out_specs=(vmem, vmem),
        scratch_shapes=[
            narrow(8, features, features),
            narrow(features, features),
            narrow(features, LANES),
            narrow(LANES, features),
            narrow(tokens, features),
            narrow(chunks, levels, columns, features),
            narrow(chunks, levels, columns, features),
            narrow(chunks, levels, columns, features),
            narrow(chunks, size, features),
            narrow(4, chunks, size, features),
            narrow(tokens, features),
            narrow(blocks, PATCH, features),
            narrow(blocks, features, PATCH),
            narrow(features, tokens),
            narrow(features // grain, grain, features),
            narrow(features // grain // 2, grain, features),
            narrow(features // grain // 2, grain, features),
            narrow((cycle // 2 - 1) * share // grain, grain, features),
            narrow(levels, share // levels, features),
            narrow(levels - 1, share // levels, features),
            narrow(levels, share // levels, features),
            pltpu.VMEM((patches * pairs * 2, 1, PATCH), jnp.float32),
            pltpu.VMEM((patches * pairs * 2, 1, PATCH), jnp.float32),
            pltpu.VMEM((patches * pairs * 2, HD, PATCH), jnp.float32),
            dma(9),
            dma(chunks, levels - 1),
            dma(chunks, levels - 1),
            dma(chunks, levels - 1),
            dma(chunks, levels - 1),
            dma(chunks, 4),
            dma(chunks, 4),
            dma(features // grain // 2),
            dma(features // grain // 2),
            dma(features // grain // 2),
            dma((cycle // 2 - 1) * share // grain),
            dma(levels - 1),
            dma(levels - 1),
            dma(levels - 1),
            dma(levels - 1),
        ],
        compiler_params=pltpu.CompilerParams(
            collective_id=0, has_side_effects=True, vmem_limit_bytes=VMEM_LIMIT
        ),
        name="whole_block",
    )(x, norm_vert, norm_patch, query_vert, keys_vert, values_vert, out_vert, query_patch, keys_patch,
      values_patch, out_patch, cotangent[0], jnp.transpose(level_bias, (1, 2, 0)), patch_bias.T, neighbours, counts)
    return (out[None], grad)


def solution(mesh):
    split = P("level", "space", None)
    return jax.shard_map(
        body,
        mesh=mesh,
        in_specs=(split,) + (P(),) * 12 + (P("space", None), P("space"), split),
        out_specs=(split, P("space", None)),
        check_vma=False,
    )
```

```python
import functools
import math

import jax
import jax.numpy as jnp
from jax import lax
from jax.experimental import pallas as pl
from jax.experimental.pallas import tpu as pltpu
from jax.sharding import PartitionSpec as P

HD = 64
PATCH = 256
LANES = 128
ROWS = 16
DEPTH = 3
STRIPS = 2
WIDE = 2
VMEM_LIMIT = 58 * 1024 * 1024

epsilon = 1e-06


def normalized(widened, scaling):
    mean_square = jnp.mean(widened * widened, axis=-1, keepdims=True)
    return (widened * lax.rsqrt(mean_square + epsilon) * scaling).astype(jnp.bfloat16)


def project(inputs, weight):
    return jnp.dot(inputs, weight, preferred_element_type=jnp.float32).astype(jnp.bfloat16)


def vertical(x, gain, wq, wk, wv, wo, bias_rows, gather_heads, spread_heads):
    levels, columns, features = x.shape
    tokens = levels * columns
    x = x.reshape(tokens, features).astype(jnp.float32)
    normed = normalized(x, gain)
    queries = project(normed, wq).astype(jnp.float32)
    keys = project(normed, wk).astype(jnp.float32)
    values = project(normed, wv).astype(jnp.float32)
    part = lambda array, i: array[i * columns : (i + 1) * columns]
    products = jnp.concatenate(
        [(part(queries, i) * part(keys, j)).astype(jnp.bfloat16) for i in range(levels) for j in range(levels)], axis=0
    )
    summed = jnp.dot(products, gather_heads, preferred_element_type=jnp.float32) * HD ** (-0.5)
    weights = []
    for i in range(levels):
        scores = [part(summed, i * levels + j) + bias_rows[i * levels + j] for j in range(levels)]
        top = functools.reduce(jnp.maximum, scores)
        raised = [jnp.exp(score - top) for score in scores]
        inverse = 1.0 / functools.reduce(jnp.add, raised)
        weights += [(each * inverse).astype(jnp.bfloat16) for each in raised]
    spread = jnp.dot(jnp.concatenate(weights, axis=0), spread_heads, preferred_element_type=jnp.float32)
    mixed = [
        functools.reduce(jnp.add, [part(spread, i * levels + j) * part(values, j) for j in range(levels)])
        for i in range(levels)
    ]
    attn = jnp.concatenate(mixed, axis=0).astype(jnp.bfloat16)
    hidden = x + jnp.dot(attn, wo, preferred_element_type=jnp.float32)
    return hidden.astype(jnp.bfloat16).reshape(levels, columns, features)


def choices(nb_ref, count_ref, patch, source, per_device):
    live = jnp.int32(0)
    within = jnp.int32(0)
    for m in range(nb_ref.shape[1]):
        listed = jnp.maximum(nb_ref[patch, m], 0)
        hit = jnp.logical_and(m < count_ref[patch], lax.div(listed, per_device) == source)
        live = jnp.where(hit, 1, live)
        within = jnp.where(hit, lax.rem(listed, per_device), within)
    return live, within


def score(step, patch, parity, parts, q_ref, k_ref):
    low = lax.broadcasted_iota(jnp.int32, (1, LANES), 1) < HD
    mine = low if parity == 0 else jnp.logical_not(low)
    lanes = pl.ds(pl.multiple_of(step * LANES, LANES), LANES)
    query = q_ref[pl.ds(patch * PATCH, PATCH), lanes]
    query = jnp.where(mine, query, jnp.zeros_like(query))
    keys = jnp.concatenate([k_ref[block, pl.ds(first, count), lanes] for block, first, count, _ in parts], axis=0)
    return lax.dot_general(keys, query, (((1,), (1,)), ((), ())), preferred_element_type=jnp.float32)


def soften(scores, parts, before):
    pieces, at = [], 0
    for _, _, count, add in parts:
        pieces.append((scores[at : at + count], add))
        at += count
    top = functools.reduce(jnp.maximum, [jnp.max(s, axis=0, keepdims=True) + a for s, a in pieces])
    if before is not None:
        top = jnp.maximum(top, before)
    raised = [jnp.exp2(s + (a - top)) for s, a in pieces]
    total = functools.reduce(jnp.add, [jnp.sum(r, axis=0, keepdims=True) for r in raised])
    return top, total, jnp.concatenate([r.astype(jnp.bfloat16) for r in raised], axis=0)


def mix(step, parity, raised, parts, vt_ref):
    rows = pl.ds(pl.multiple_of(step * LANES + parity * HD, HD), HD)
    values = jnp.concatenate([vt_ref[block, rows, pl.ds(first, count)] for block, first, count, _ in parts], axis=1)
    return jnp.dot(values, raised, preferred_element_type=jnp.float32)


def attend(steps, patches, second, parts_of, q_ref, k_ref, vt_ref, top_ref, finish):
    heads = [(step, patch, parity) for step in steps for patch in range(patches) for parity in range(2)]
    parts = [parts_of(patch, step * 2 + parity, second) for step, patch, parity in heads]
    slots = [patch * top_ref.shape[0] // patches + step * 2 + parity for step, patch, parity in heads]
    befores = [top_ref[slot] if second else None for slot in slots]
    scores, soft = {}, {}
    for turn in range(len(heads) + 2):
        if turn < len(heads):
            scores[turn] = score(*heads[turn], parts[turn], q_ref, k_ref)
        if 1 <= turn < len(heads) + 1:
            soft[turn - 1] = soften(scores.pop(turn - 1), parts[turn - 1], befores[turn - 1])
        if turn >= 2:
            at = turn - 2
            step, patch, parity = heads[at]
            top, total, raised = soft.pop(at)
            finish(slots[at], patch, parity, befores[at], top, total, mix(step, parity, raised, parts[at], vt_ref))


def remote(src, dst, send, recv, device):
    return pltpu.make_async_remote_copy(
        src_ref=src, dst_ref=dst, send_sem=send, recv_sem=recv, device_id=device,
        device_id_type=pl.DeviceIdType.MESH,
    )


def whole_kernel(cycle, levels, x_ref, nv_ref, np_ref, wqv_hbm, wkv_hbm, wvv_hbm, wov_hbm, wqp_hbm, wkp_hbm, wvp_hbm,
                 wop_hbm, cot_hbm, lb_ref, pb_ref, nb_ref, count_ref, out_ref, grad_ref, block_ref, weight_ref, wvt_ref, gather_ref,
                 spread_ref, cot_ref, in_ref, hsend_ref, hid_ref, own_ref, far_ref, q_ref, k_ref, vt_ref, attn_ref,
                 gsend_ref, gpair_ref, gsum_ref, grecv_ref, lsend_ref, lrecv_ref, final_ref, top_ref, total_ref, mixed_ref, load_sem, in_send,
                 in_recv, back_send, back_recv, halo_send, halo_recv, pair_send, pair_recv, share_send, share_recv, part_send, part_recv,
                 full_send, full_recv):
    chunks, _, columns, features = x_ref.shape
    size = levels * columns
    split = PATCH // size
    patches = chunks // split
    half = max(LANES, size)
    group = half // size
    order = [patch * split + turn for turn in range(split) for patch in range(patches)]
    place = lax.axis_index("space")
    level = lax.axis_index("level")
    weights_hbm = (wqv_hbm, wkv_hbm, wvv_hbm, wov_hbm, wqp_hbm, wkp_hbm, wvp_hbm, wop_hbm)
    loads = [pltpu.make_async_copy(w, weight_ref.at[i], load_sem.at[i]) for i, w in enumerate(weights_hbm)]
    loads.append(pltpu.make_async_copy(cot_hbm, cot_ref, load_sem.at[len(weights_hbm)]))
    for load in loads:
        load.start()

    barrier = pltpu.get_barrier_semaphore()
    peers = [lax.rem(level + k, levels) for k in range(1, levels)]
    around = [lax.rem(place + k, cycle) for k in range(1, cycle)]
    for peer in peers:
        pl.semaphore_signal(barrier, inc=1, device_id={"level": peer}, device_id_type=pl.DeviceIdType.MESH)
    for peer in around:
        pl.semaphore_signal(barrier, inc=1, device_id={"space": peer}, device_id_type=pl.DeviceIdType.MESH)
    pl.semaphore_wait(barrier, levels - 1 + cycle - 1)

    inward, back, sent = [], [], []

    def send_in(i):
        c = order[i]
        steps = []
        for k, peer in enumerate(peers):
            steps.append(remote(x_ref.at[c, peer], in_ref.at[c, level], in_send.at[c, k], in_recv.at[c, k],
                                {"level": peer}))
            steps[-1].start()
        in_ref[c, level] = x_ref[c, level]
        inward.append(steps)

    for i in range(min(DEPTH, chunks)):
        send_in(i)

    lane = lax.broadcasted_iota(jnp.int32, (1, LANES), 1)
    bias_rows = []
    for i in range(levels):
        for j in range(levels):
            row = jnp.zeros((1, LANES), jnp.float32)
            for h in range(lb_ref.shape[2]):
                row = jnp.where(lane == h, lb_ref[i, j, h], row)
            bias_rows.append(row)
    head_of = lax.broadcasted_iota(jnp.int32, (features, LANES), 0) // HD
    gather_ref[...] = (head_of == lax.broadcasted_iota(jnp.int32, (features, LANES), 1)).astype(jnp.bfloat16)
    head_to = lax.broadcasted_iota(jnp.int32, (LANES, features), 1) // HD
    spread_ref[...] = (head_to == lax.broadcasted_iota(jnp.int32, (LANES, features), 0)).astype(jnp.bfloat16)
    for load in loads[:4]:
        load.wait()

    def vertical_step(i):
        c = order[i]
        for step in inward[i]:
            step.wait_recv()
        hsend_ref[c] = vertical(in_ref[c], nv_ref[...][None], weight_ref[0], weight_ref[1], weight_ref[2],
                                weight_ref[3], bias_rows, gather_ref[...], spread_ref[...])
        steps = []
        for k, peer in enumerate(peers):
            steps.append(remote(hsend_ref.at[c, peer], hid_ref.at[c, level], back_send.at[c, k], back_recv.at[c, k],
                                {"level": peer}))
            steps[-1].start()
        hid_ref[c, level] = hsend_ref[c, level]
        back.append(steps)
        if i + DEPTH < chunks:
            send_in(i + DEPTH)
        if i == 0:
            for load in loads[4:]:
                load.wait()
            wvt_ref[...] = weight_ref[6].T

    chips = cycle // 2
    chip, core = lax.div(place, 2), lax.rem(place, 2)
    toward = core * 2 - 1
    sources = [lax.rem(place + step * toward + 2 * cycle, cycle) for step in (1, 2, -1, -2)]
    partner = sources[2]
    far = len(sources) * patches
    scale = HD ** (-0.5) * math.log2(math.e)
    relayed = chips == 4
    odd = lax.rem(chip + core, 2)
    near, diagonal = (3 - 2 * odd, 1 + 2 * odd) if relayed else (1, 3)
    beside = (chip + 1 - 2 * lax.rem(chip, 2)) * 2 + core
    across = lax.rem(chip + 2, chips) * 2 + core

    def halo_copy(c, src, slot, lane_of, device):
        return remote(src, far_ref.at[slot, c], halo_send.at[c, lane_of], halo_recv.at[c, slot], {"space": device})

    def begin(make):
        make().start()
        sent.append(make)

    def halo_step(i):
        c = order[i]
        for step in back[i]:
            step.wait_recv()
        own_ref[c] = normalized(hid_ref[c].reshape(size, features).astype(jnp.float32), np_ref[...][None])
        if relayed:
            begin(lambda: halo_copy(c, own_ref.at[c], diagonal, 0, beside))
        else:
            begin(lambda: halo_copy(c, own_ref.at[c], 3, 0, sources[1]))
            begin(lambda: halo_copy(c, own_ref.at[c], 1, 2, sources[3]))
        begin(lambda: halo_copy(c, own_ref.at[c], 2, 1, partner))

    def relay_step(i):
        c = order[i]
        halo_copy(c, own_ref.at[c], near, 0, beside).wait_recv()
        if relayed:
            begin(lambda: halo_copy(c, far_ref.at[near, c], diagonal, 2, across))

    def forward_step(i):
        c = order[i]
        halo_copy(c, own_ref.at[c], diagonal, 0, across).wait_recv()
        begin(lambda: halo_copy(c, far_ref.at[3, c], 0, 3, partner))

    def members(patch, part):
        return [patch * split + part * group + k for k in range(group)]

    def keys_values(normed, blocks, part):
        keys = project(normed, weight_ref[5])
        values = lax.dot_general(
            wvt_ref[...], normed, (((1,), (1,)), ((), ())), preferred_element_type=jnp.float32
        ).astype(jnp.bfloat16)
        for k, block in enumerate(blocks):
            k_ref[block, part * half : (part + 1) * half, :] = keys[k * half : (k + 1) * half]
            vt_ref[block, :, part * half : (part + 1) * half] = values[:, k * half : (k + 1) * half]

    def own_half(patch, part):
        first = members(patch, part)[0]
        normed = own_ref[first : first + group].reshape(half, features)
        queries = jnp.dot(normed, weight_ref[4], preferred_element_type=jnp.float32) * scale
        q_ref[first * size : first * size + half, :] = queries.astype(jnp.bfloat16)
        keys_values(normed, (far + patch,), part)

    def far_half(slots, patch, part):
        first = members(patch, part)[0]
        for slot in slots:
            if slot in (0, 2):
                for c in members(patch, part):
                    halo_copy(c, own_ref.at[c], slot, 1, partner).wait_recv()
        normed = jnp.concatenate([far_ref[slot, first : first + group].reshape(half, features) for slot in slots], axis=0)
        keys_values(normed, [slot * patches + patch for slot in slots], part)

    halves = PATCH // half
    arrival = [i + 2.4 if i < chunks - 2 else chunks - 0.6 + 0.5 * (i - chunks + 3) for i in range(chunks)]
    events = []
    for i in range(chunks):
        events.append((float(i), vertical_step, (i,)))
        events.append((arrival[i], halo_step, (i,)))
        events.append((arrival[i] + 0.9, relay_step, (i,)))
        events.append((arrival[i] + 1.8, forward_step, (i,)))
    for patch in range(patches):
        for part in range(halves):
            last = order.index(members(patch, part)[-1])
            events.append((arrival[last] + 0.05, own_half, (patch, part)))
            events.append((arrival[last] + 0.35, far_half, ((2,), patch, part)))
            events.append((arrival[last] + 2.2, far_half, ((1, 3, 0), patch, part)))
    events.sort(key=lambda event: event[0])
    start = arrival[-1] + 0.5
    pairs = features // LANES
    late = [event for event in events if event[0] > start]
    for _, act, args in events:
        if _ <= start:
            act(*args)
    tables = [[choices(nb_ref, count_ref, patch, source, patches) for source in sources] for patch in range(patches)]

    def parts_of(patch, head, second):
        log2e = jnp.float32(math.log2(math.e))
        adds = [jnp.where(live > 0, pb_ref[1, head], jnp.float32(-1e30)) * log2e for live, _ in tables[patch]]
        block = [slot * patches + tables[patch][slot][1] for slot in range(len(sources))]
        count = PATCH - half
        if second:
            return [(block[slot], count, half, adds[slot]) for slot in (0, 1, 3)]
        own = [(far + patch, 0, PATCH, pb_ref[0, head] * log2e), (block[2], 0, PATCH, adds[2])]
        return own + [(block[slot], 0, count, adds[slot]) for slot in (0, 1, 3)]

    inside = [event for event in late if event[1] in (relay_step, forward_step)][:3]
    after = [event for event in late if event not in inside]

    def early_pair(turn, carry):
        steps = [turn * WIDE + k for k in range(WIDE)]
        for when, (_, act, args) in zip((1, 2, 2), inside):

            @pl.when(turn == when)
            def _():
                act(*args)

        def finish(slot, patch, parity, before, top, total, mixed):
            top_ref[slot] = top
            total_ref[slot] = total
            mixed_ref[slot] = mixed

        attend(steps, patches, False, parts_of, q_ref, k_ref, vt_ref, top_ref, finish)
        return carry

    lax.fori_loop(0, pairs // WIDE, early_pair, 0)
    for _, act, args in after:
        act(*args)

    share = features // cycle
    grain = gsend_ref.shape[1]
    per_pair = LANES // grain
    per_owner = share // grain

    def pair_copy(index):
        slot = lax.div(index, 2 * per_owner) * per_owner + lax.rem(index, per_owner)
        return slot, remote(gsend_ref.at[index], gpair_ref.at[slot], pair_send.at[slot], pair_recv.at[slot],
                            {"space": partner})

    def share_copy(slot):
        owner = lax.div(slot, per_owner)
        gap = lax.rem(chip - owner + chips, chips)
        there = jnp.maximum(gap - 1, 0) * per_owner + lax.rem(slot, per_owner)
        return owner, remote(gsum_ref.at[slot], grecv_ref.at[there], share_send.at[slot], share_recv.at[there],
                             {"space": owner * 2 + core})

    def gather_pair(step):
        for part in range(per_pair):
            index = step * per_pair + part

            @pl.when(lax.rem(lax.div(index, per_owner), 2) == core)
            def _():
                slot, copy = pair_copy(index)
                copy.wait_recv()
                both = gsend_ref[index].astype(jnp.float32) + gpair_ref[slot].astype(jnp.float32)
                gsum_ref[slot] = both.astype(jnp.bfloat16)
                owner, copy = share_copy(slot)

                @pl.when(owner != chip)
                def _():
                    copy.start()

    def step_of(turn):
        return lax.rem(lax.div(chip * pairs, chips) + 2 + turn, pairs)

    def pair(turn, carry):
        step = step_of(turn)

        def finish(slot, patch, parity, before, top, total, mixed):
            fade = jnp.exp2(before - top)
            mixed = (mixed + mixed_ref[slot] * fade) * (1.0 / (total + total_ref[slot] * fade))
            rows = pl.ds(pl.multiple_of(step * LANES + parity * HD, HD), HD)
            attn_ref[rows, patch * PATCH : (patch + 1) * PATCH] = mixed.astype(jnp.bfloat16)

        attend([step], patches, True, parts_of, q_ref, k_ref, vt_ref, top_ref, finish)
        rows = pl.ds(pl.multiple_of(step * LANES, LANES), LANES)
        total = jnp.dot(attn_ref[rows, :], cot_ref[...], preferred_element_type=jnp.float32).astype(jnp.bfloat16)
        for part in range(per_pair):
            gsend_ref[step * per_pair + part] = total[part * grain : (part + 1) * grain]
        for part in range(per_pair):
            index = step * per_pair + part

            @pl.when(lax.rem(lax.div(index, per_owner), 2) != core)
            def _():
                pair_copy(index)[1].start()

        @pl.when(turn > 0)
        def _():
            gather_pair(step_of(turn - 1))

        return carry

    lax.fori_loop(0, pairs, pair, 0)
    gather_pair(step_of(pairs - 1))
    mixture = lax.dot_general(
        attn_ref[...], weight_ref[7], (((0,), (0,)), ((), ())), preferred_element_type=jnp.float32
    )
    block_ref[...] = (hid_ref[...].reshape(patches * PATCH, features).astype(jnp.float32) + mixture).astype(jnp.bfloat16)
    write = pltpu.make_async_copy(block_ref, out_ref, load_sem.at[0])
    write.start()
    sums = []
    for part in range(per_owner):
        sums.append(gsum_ref[chip * per_owner + part].astype(jnp.float32))
        for k in range(chips - 1):
            slot = k * per_owner + part
            remote(gsum_ref.at[0], grecv_ref.at[slot], share_send.at[0], share_recv.at[slot],
                   {"space": partner}).wait_recv()
            sums[-1] = sums[-1] + grecv_ref[slot].astype(jnp.float32)
    gathered = jnp.concatenate(sums, axis=0)
    piece = share // levels
    strips = lsend_ref.shape[0]
    width = features // strips
    for strip in range(strips):
        for i in range(levels):
            lsend_ref[strip, i] = gathered[
                i * piece : (i + 1) * piece, strip * width : (strip + 1) * width
            ].astype(jnp.bfloat16)
    parts, fulls = [], []
    for strip in range(strips):
        for k, peer in enumerate(peers):
            parts.append(remote(lsend_ref.at[strip, peer], lrecv_ref.at[strip, k], part_send.at[strip, k],
                                part_recv.at[strip, k], {"level": peer}))
            parts[-1].start()
    for steps in inward + back + [[make() for make in sent]]:
        for step in steps:
            step.wait_send()

    def drained(slot, carry):
        index = lax.div(slot, per_owner) * 2 * per_owner + (1 - core) * per_owner + lax.rem(slot, per_owner)
        pair_copy(index)[1].wait_send()
        owner, copy = share_copy(slot)

        @pl.when(owner != chip)
        def _():
            copy.wait_send()

        return carry

    lax.fori_loop(0, chips * per_owner, drained, 0)

    for strip in range(strips):
        gathered = lsend_ref[strip, level].astype(jnp.float32)
        for k in range(levels - 1):
            parts[strip * (levels - 1) + k].wait_recv()
            gathered = gathered + lrecv_ref[strip, k].astype(jnp.float32)
        final_ref[strip, level] = gathered.astype(jnp.bfloat16)
        for k, peer in enumerate(peers):
            fulls.append(remote(final_ref.at[strip, level], final_ref.at[strip, level], full_send.at[strip, k],
                                full_recv.at[strip, k], {"level": peer}))
            fulls[-1].start()
    for step in fulls:
        step.wait_recv()
    for strip in range(strips):
        for i in range(levels):
            grad_ref[i * piece : (i + 1) * piece, strip * width : (strip + 1) * width] = final_ref[strip, i].astype(
                jnp.float32
            )
    for step in parts + fulls:
        step.wait_send()
    write.wait()


def body(fields, norm_vert, query_vert, keys_vert, values_vert, out_vert, level_bias, norm_patch, query_patch,
         keys_patch, values_patch, out_patch, patch_bias, neighbours, counts, cotangent):
    _, tokens, features = fields.shape
    levels = lax.axis_size("level")
    cycle = lax.axis_size("space")
    patches = tokens // PATCH
    columns = ROWS
    size = levels * columns
    chunks = tokens // size
    pairs = features // LANES
    grain = math.gcd(features // cycle, LANES)
    share = features // cycle
    x = fields.reshape(chunks, levels, columns, features)
    vmem = pl.BlockSpec(memory_space=pltpu.VMEM)
    smem = pl.BlockSpec(memory_space=pltpu.SMEM)
    hbm = pl.BlockSpec(memory_space=pl.ANY)
    narrow = lambda *shape: pltpu.VMEM(shape, jnp.bfloat16)
    dma = lambda *shape: pltpu.SemaphoreType.DMA(shape)
    blocks = 5 * patches
    out, grad = pl.pallas_call(
        functools.partial(whole_kernel, cycle, levels),
        out_shape=(
            jax.ShapeDtypeStruct((tokens, features), jnp.bfloat16),
            jax.ShapeDtypeStruct((share, features), jnp.float32),
        ),
        in_specs=[vmem] * 3 + [hbm] * 9 + [smem] * 4,
        out_specs=(hbm, vmem),
        scratch_shapes=[
            narrow(tokens, features),
            narrow(8, features, features),
            narrow(features, features),
            narrow(features, LANES),
            narrow(LANES, features),
            narrow(tokens, features),
            narrow(chunks, levels, columns, features),
            narrow(chunks, levels, columns, features),
            narrow(chunks, levels, columns, features),
            narrow(chunks, size, features),
            narrow(4, chunks, size, features),
            narrow(tokens, features),
            narrow(blocks, PATCH, features),
            narrow(blocks, features, PATCH),
            narrow(features, tokens),
            narrow(features // grain, grain, features),
            narrow(features // grain // 2, grain, features),
            narrow(features // grain // 2, grain, features),
            narrow((cycle // 2 - 1) * share // grain, grain, features),
            narrow(STRIPS, levels, share // levels, features // STRIPS),
            narrow(STRIPS, levels - 1, share // levels, features // STRIPS),
            narrow(STRIPS, levels, share // levels, features // STRIPS),
            pltpu.VMEM((patches * pairs * 2, 1, PATCH), jnp.float32),
            pltpu.VMEM((patches * pairs * 2, 1, PATCH), jnp.float32),
            pltpu.VMEM((patches * pairs * 2, HD, PATCH), jnp.float32),
            dma(9),
            dma(chunks, levels - 1),
            dma(chunks, levels - 1),
            dma(chunks, levels - 1),
            dma(chunks, levels - 1),
            dma(chunks, 4),
            dma(chunks, 4),
            dma(features // grain // 2),
            dma(features // grain // 2),
            dma(features // grain // 2),
            dma((cycle // 2 - 1) * share // grain),
            dma(STRIPS, levels - 1),
            dma(STRIPS, levels - 1),
            dma(STRIPS, levels - 1),
            dma(STRIPS, levels - 1),
        ],
        compiler_params=pltpu.CompilerParams(
            collective_id=0, has_side_effects=True, vmem_limit_bytes=VMEM_LIMIT
        ),
        name="whole_block",
    )(x, norm_vert, norm_patch, query_vert, keys_vert, values_vert, out_vert, query_patch, keys_patch,
      values_patch, out_patch, cotangent[0], jnp.transpose(level_bias, (1, 2, 0)), patch_bias.T, neighbours, counts)
    return (out[None], grad)


def solution(mesh):
    split = P("level", "space", None)
    return jax.shard_map(
        body,
        mesh=mesh,
        in_specs=(split,) + (P(),) * 12 + (P("space", None), P("space"), split),
        out_specs=(split, P("space", None)),
        check_vma=False,
    )
```

```python
import functools
import math

import jax
import jax.numpy as jnp
from jax import lax
from jax.experimental import pallas as pl
from jax.experimental.pallas import tpu as pltpu
from jax.sharding import PartitionSpec as P

HD = 64
PATCH = 256
LANES = 128
ROWS = 16
DEPTH = 3
STRIPS = 2
WIDE = 2
VMEM_LIMIT = 58 * 1024 * 1024

epsilon = 1e-06


def normalized(widened, scaling):
    mean_square = jnp.mean(widened * widened, axis=-1, keepdims=True)
    return (widened * lax.rsqrt(mean_square + epsilon) * scaling).astype(jnp.bfloat16)


def project(inputs, weight):
    return jnp.dot(inputs, weight, preferred_element_type=jnp.float32).astype(jnp.bfloat16)


def vertical(x, gain, wq, wk, wv, wo, bias_rows, gather_heads, spread_heads):
    levels, columns, features = x.shape
    tokens = levels * columns
    x = x.reshape(tokens, features).astype(jnp.float32)
    normed = normalized(x, gain)
    queries = project(normed, wq).astype(jnp.float32)
    keys = project(normed, wk).astype(jnp.float32)
    values = project(normed, wv).astype(jnp.float32)
    part = lambda array, i: array[i * columns : (i + 1) * columns]
    products = jnp.concatenate(
        [(part(queries, i) * part(keys, j)).astype(jnp.bfloat16) for i in range(levels) for j in range(levels)], axis=0
    )
    summed = jnp.dot(products, gather_heads, preferred_element_type=jnp.float32) * HD ** (-0.5)
    weights = []
    for i in range(levels):
        scores = [part(summed, i * levels + j) + bias_rows[i * levels + j] for j in range(levels)]
        top = functools.reduce(jnp.maximum, scores)
        raised = [jnp.exp(score - top) for score in scores]
        inverse = 1.0 / functools.reduce(jnp.add, raised)
        weights += [(each * inverse).astype(jnp.bfloat16) for each in raised]
    spread = jnp.dot(jnp.concatenate(weights, axis=0), spread_heads, preferred_element_type=jnp.float32)
    mixed = [
        functools.reduce(jnp.add, [part(spread, i * levels + j) * part(values, j) for j in range(levels)])
        for i in range(levels)
    ]
    attn = jnp.concatenate(mixed, axis=0).astype(jnp.bfloat16)
    hidden = x + jnp.dot(attn, wo, preferred_element_type=jnp.float32)
    return hidden.astype(jnp.bfloat16).reshape(levels, columns, features)


def choices(nb_ref, count_ref, patch, source, per_device):
    live = jnp.int32(0)
    within = jnp.int32(0)
    for m in range(nb_ref.shape[1]):
        listed = jnp.maximum(nb_ref[patch, m], 0)
        hit = jnp.logical_and(m < count_ref[patch], lax.div(listed, per_device) == source)
        live = jnp.where(hit, 1, live)
        within = jnp.where(hit, lax.rem(listed, per_device), within)
    return live, within


def score(step, patch, parity, parts, q_ref, k_ref):
    low = lax.broadcasted_iota(jnp.int32, (1, LANES), 1) < HD
    mine = low if parity == 0 else jnp.logical_not(low)
    lanes = pl.ds(pl.multiple_of(step * LANES, LANES), LANES)
    query = q_ref[pl.ds(patch * PATCH, PATCH), lanes]
    query = jnp.where(mine, query, jnp.zeros_like(query))
    keys = jnp.concatenate([k_ref[block, pl.ds(first, count), lanes] for block, first, count, _ in parts], axis=0)
    return lax.dot_general(keys, query, (((1,), (1,)), ((), ())), preferred_element_type=jnp.float32)


def soften(scores, parts, before):
    pieces, at = [], 0
    for _, _, count, add in parts:
        pieces.append((scores[at : at + count], add))
        at += count
    top = functools.reduce(jnp.maximum, [jnp.max(s, axis=0, keepdims=True) + a for s, a in pieces])
    if before is not None:
        top = jnp.maximum(top, before)
    raised = [jnp.exp2(s + (a - top)) for s, a in pieces]
    return top, jnp.concatenate([r.astype(jnp.bfloat16) for r in raised], axis=0)


def mix(step, parity, raised, parts, vt_ref):
    rows = pl.ds(pl.multiple_of(step * LANES + parity * HD, HD), HD)
    values = jnp.concatenate([vt_ref[block, rows, pl.ds(first, count)] for block, first, count, _ in parts], axis=1)
    values = jnp.concatenate([values, jnp.ones((ROWS, values.shape[1]), jnp.bfloat16)], axis=0)
    mixed = jnp.dot(values, raised, preferred_element_type=jnp.float32)
    return mixed[HD : HD + 1], mixed[:HD]


def attend(steps, patches, second, parts_of, q_ref, k_ref, vt_ref, top_ref, finish):
    heads = [(step, patch, parity) for step in steps for patch in range(patches) for parity in range(2)]
    parts = [parts_of(patch, step * 2 + parity, second) for step, patch, parity in heads]
    slots = [patch * top_ref.shape[0] // patches + step * 2 + parity for step, patch, parity in heads]
    befores = [top_ref[slot] if second else None for slot in slots]
    scores, soft = {}, {}
    for turn in range(len(heads) + 2):
        if turn < len(heads):
            scores[turn] = score(*heads[turn], parts[turn], q_ref, k_ref)
        if 1 <= turn < len(heads) + 1:
            soft[turn - 1] = soften(scores.pop(turn - 1), parts[turn - 1], befores[turn - 1])
        if turn >= 2:
            at = turn - 2
            step, patch, parity = heads[at]
            top, raised = soft.pop(at)
            finish(slots[at], patch, parity, befores[at], top, *mix(step, parity, raised, parts[at], vt_ref))


def remote(src, dst, send, recv, device):
    return pltpu.make_async_remote_copy(
        src_ref=src, dst_ref=dst, send_sem=send, recv_sem=recv, device_id=device,
        device_id_type=pl.DeviceIdType.MESH,
    )


def whole_kernel(cycle, levels, x_ref, nv_ref, np_ref, wqv_hbm, wkv_hbm, wvv_hbm, wov_hbm, wqp_hbm, wkp_hbm, wvp_hbm,
                 wop_hbm, cot_hbm, lb_ref, pb_ref, nb_ref, count_ref, out_ref, grad_ref, block_ref, weight_ref, wvt_ref, gather_ref,
                 spread_ref, cot_ref, in_ref, hsend_ref, hid_ref, own_ref, far_ref, q_ref, k_ref, vt_ref, attn_ref,
                 gsend_ref, gpair_ref, gsum_ref, grecv_ref, lsend_ref, lrecv_ref, final_ref, top_ref, total_ref, mixed_ref, load_sem, in_send,
                 in_recv, back_send, back_recv, halo_send, halo_recv, pair_send, pair_recv, share_send, share_recv, part_send, part_recv,
                 full_send, full_recv):
    chunks, _, columns, features = x_ref.shape
    size = levels * columns
    split = PATCH // size
    patches = chunks // split
    half = max(LANES, size)
    group = half // size
    order = [patch * split + turn for turn in range(split) for patch in range(patches)]
    place = lax.axis_index("space")
    level = lax.axis_index("level")
    weights_hbm = (wqv_hbm, wkv_hbm, wvv_hbm, wov_hbm, wqp_hbm, wkp_hbm, wvp_hbm, wop_hbm)
    loads = [pltpu.make_async_copy(w, weight_ref.at[i], load_sem.at[i]) for i, w in enumerate(weights_hbm)]
    loads.append(pltpu.make_async_copy(cot_hbm, cot_ref, load_sem.at[len(weights_hbm)]))
    for load in loads:
        load.start()

    barrier = pltpu.get_barrier_semaphore()
    peers = [lax.rem(level + k, levels) for k in range(1, levels)]
    around = [lax.rem(place + k, cycle) for k in range(1, cycle)]
    for peer in peers:
        pl.semaphore_signal(barrier, inc=1, device_id={"level": peer}, device_id_type=pl.DeviceIdType.MESH)
    for peer in around:
        pl.semaphore_signal(barrier, inc=1, device_id={"space": peer}, device_id_type=pl.DeviceIdType.MESH)
    pl.semaphore_wait(barrier, levels - 1 + cycle - 1)

    inward, back, sent = [], [], []

    def send_in(i):
        c = order[i]
        steps = []
        for k, peer in enumerate(peers):
            steps.append(remote(x_ref.at[c, peer], in_ref.at[c, level], in_send.at[c, k], in_recv.at[c, k],
                                {"level": peer}))
            steps[-1].start()
        in_ref[c, level] = x_ref[c, level]
        inward.append(steps)

    for i in range(min(DEPTH, chunks)):
        send_in(i)

    lane = lax.broadcasted_iota(jnp.int32, (1, LANES), 1)
    bias_rows = []
    for i in range(levels):
        for j in range(levels):
            row = jnp.zeros((1, LANES), jnp.float32)
            for h in range(lb_ref.shape[2]):
                row = jnp.where(lane == h, lb_ref[i, j, h], row)
            bias_rows.append(row)
    head_of = lax.broadcasted_iota(jnp.int32, (features, LANES), 0) // HD
    gather_ref[...] = (head_of == lax.broadcasted_iota(jnp.int32, (features, LANES), 1)).astype(jnp.bfloat16)
    head_to = lax.broadcasted_iota(jnp.int32, (LANES, features), 1) // HD
    spread_ref[...] = (head_to == lax.broadcasted_iota(jnp.int32, (LANES, features), 0)).astype(jnp.bfloat16)
    for load in loads[:4]:
        load.wait()

    def vertical_step(i):
        c = order[i]
        for step in inward[i]:
            step.wait_recv()
        hsend_ref[c] = vertical(in_ref[c], nv_ref[...][None], weight_ref[0], weight_ref[1], weight_ref[2],
                                weight_ref[3], bias_rows, gather_ref[...], spread_ref[...])
        steps = []
        for k, peer in enumerate(peers):
            steps.append(remote(hsend_ref.at[c, peer], hid_ref.at[c, level], back_send.at[c, k], back_recv.at[c, k],
                                {"level": peer}))
            steps[-1].start()
        hid_ref[c, level] = hsend_ref[c, level]
        back.append(steps)
        if i + DEPTH < chunks:
            send_in(i + DEPTH)
        if i == 0:
            for load in loads[4:]:
                load.wait()
            wvt_ref[...] = weight_ref[6].T

    chips = cycle // 2
    chip, core = lax.div(place, 2), lax.rem(place, 2)
    toward = core * 2 - 1
    sources = [lax.rem(place + step * toward + 2 * cycle, cycle) for step in (1, 2, -1, -2)]
    partner = sources[2]
    far = len(sources) * patches
    scale = HD ** (-0.5) * math.log2(math.e)
    relayed = chips == 4
    odd = lax.rem(chip + core, 2)
    near, diagonal = (3 - 2 * odd, 1 + 2 * odd) if relayed else (1, 3)
    beside = (chip + 1 - 2 * lax.rem(chip, 2)) * 2 + core
    across = lax.rem(chip + 2, chips) * 2 + core

    def halo_copy(c, src, slot, lane_of, device):
        return remote(src, far_ref.at[slot, c], halo_send.at[c, lane_of], halo_recv.at[c, slot], {"space": device})

    def begin(make):
        make().start()
        sent.append(make)

    def halo_step(i):
        c = order[i]
        for step in back[i]:
            step.wait_recv()
        own_ref[c] = normalized(hid_ref[c].reshape(size, features).astype(jnp.float32), np_ref[...][None])
        if relayed:
            begin(lambda: halo_copy(c, own_ref.at[c], diagonal, 0, beside))
        else:
            begin(lambda: halo_copy(c, own_ref.at[c], 3, 0, sources[1]))
            begin(lambda: halo_copy(c, own_ref.at[c], 1, 2, sources[3]))
        begin(lambda: halo_copy(c, own_ref.at[c], 2, 1, partner))

    def relay_step(i):
        c = order[i]
        halo_copy(c, own_ref.at[c], near, 0, beside).wait_recv()
        if relayed:
            begin(lambda: halo_copy(c, far_ref.at[near, c], diagonal, 2, across))

    def forward_step(i):
        c = order[i]
        halo_copy(c, own_ref.at[c], diagonal, 0, across).wait_recv()
        begin(lambda: halo_copy(c, far_ref.at[3, c], 0, 3, partner))

    def members(patch, part):
        return [patch * split + part * group + k for k in range(group)]

    def keys_values(normed, blocks, part):
        keys = project(normed, weight_ref[5])
        values = lax.dot_general(
            wvt_ref[...], normed, (((1,), (1,)), ((), ())), preferred_element_type=jnp.float32
        ).astype(jnp.bfloat16)
        for k, block in enumerate(blocks):
            k_ref[block, part * half : (part + 1) * half, :] = keys[k * half : (k + 1) * half]
            vt_ref[block, :, part * half : (part + 1) * half] = values[:, k * half : (k + 1) * half]

    def own_half(patch, part):
        first = members(patch, part)[0]
        normed = own_ref[first : first + group].reshape(half, features)
        queries = jnp.dot(normed, weight_ref[4], preferred_element_type=jnp.float32) * scale
        q_ref[first * size : first * size + half, :] = queries.astype(jnp.bfloat16)
        keys_values(normed, (far + patch,), part)

    def far_half(slots, patch, part):
        first = members(patch, part)[0]
        for slot in slots:
            if slot in (0, 2):
                for c in members(patch, part):
                    halo_copy(c, own_ref.at[c], slot, 1, partner).wait_recv()
        normed = jnp.concatenate([far_ref[slot, first : first + group].reshape(half, features) for slot in slots], axis=0)
        keys_values(normed, [slot * patches + patch for slot in slots], part)

    halves = PATCH // half
    arrival = [i + 2.4 if i < chunks - 2 else chunks - 0.6 + 0.5 * (i - chunks + 3) for i in range(chunks)]
    events = []
    for i in range(chunks):
        events.append((float(i), vertical_step, (i,)))
        events.append((arrival[i], halo_step, (i,)))
        events.append((arrival[i] + 0.9, relay_step, (i,)))
        events.append((arrival[i] + 1.8, forward_step, (i,)))
    for patch in range(patches):
        for part in range(halves):
            last = order.index(members(patch, part)[-1])
            events.append((arrival[last] + 0.05, own_half, (patch, part)))
            events.append((arrival[last] + 0.35, far_half, ((2,), patch, part)))
            events.append((arrival[last] + 2.2, far_half, ((1, 3, 0), patch, part)))
    events.sort(key=lambda event: event[0])
    start = arrival[-1] + 0.5
    pairs = features // LANES
    late = [event for event in events if event[0] > start]
    for _, act, args in events:
        if _ <= start:
            act(*args)
    tables = [[choices(nb_ref, count_ref, patch, source, patches) for source in sources] for patch in range(patches)]

    def parts_of(patch, head, second):
        log2e = jnp.float32(math.log2(math.e))
        adds = [jnp.where(live > 0, pb_ref[1, head], jnp.float32(-1e30)) * log2e for live, _ in tables[patch]]
        block = [slot * patches + tables[patch][slot][1] for slot in range(len(sources))]
        count = PATCH - half
        if second:
            return [(block[slot], count, half, adds[slot]) for slot in (0, 1, 3)]
        own = [(far + patch, 0, PATCH, pb_ref[0, head] * log2e), (block[2], 0, PATCH, adds[2])]
        return own + [(block[slot], 0, count, adds[slot]) for slot in (0, 1, 3)]

    inside = [event for event in late if event[1] in (relay_step, forward_step)][:3]
    after = [event for event in late if event not in inside]

    def early_pair(turn, carry):
        steps = [turn * WIDE + k for k in range(WIDE)]
        for when, (_, act, args) in zip((1, 2, 2), inside):

            @pl.when(turn == when)
            def _():
                act(*args)

        def finish(slot, patch, parity, before, top, total, mixed):
            top_ref[slot] = top
            total_ref[slot] = total
            mixed_ref[slot] = mixed

        attend(steps, patches, False, parts_of, q_ref, k_ref, vt_ref, top_ref, finish)
        return carry

    lax.fori_loop(0, pairs // WIDE, early_pair, 0)
    for _, act, args in after:
        act(*args)

    share = features // cycle
    grain = gsend_ref.shape[1]
    per_pair = LANES // grain
    per_owner = share // grain

    def pair_copy(index):
        slot = lax.div(index, 2 * per_owner) * per_owner + lax.rem(index, per_owner)
        return slot, remote(gsend_ref.at[index], gpair_ref.at[slot], pair_send.at[slot], pair_recv.at[slot],
                            {"space": partner})

    def share_copy(slot):
        owner = lax.div(slot, per_owner)
        gap = lax.rem(chip - owner + chips, chips)
        there = jnp.maximum(gap - 1, 0) * per_owner + lax.rem(slot, per_owner)
        return owner, remote(gsum_ref.at[slot], grecv_ref.at[there], share_send.at[slot], share_recv.at[there],
                             {"space": owner * 2 + core})

    def gather_pair(step):
        for part in range(per_pair):
            index = step * per_pair + part

            @pl.when(lax.rem(lax.div(index, per_owner), 2) == core)
            def _():
                slot, copy = pair_copy(index)
                copy.wait_recv()
                both = gsend_ref[index].astype(jnp.float32) + gpair_ref[slot].astype(jnp.float32)
                gsum_ref[slot] = both.astype(jnp.bfloat16)
                owner, copy = share_copy(slot)

                @pl.when(owner != chip)
                def _():
                    copy.start()

    def step_of(turn):
        return lax.rem(lax.div(chip * pairs, chips) + 2 + turn, pairs)

    def pair(turn, carry):
        step = step_of(turn)

        def finish(slot, patch, parity, before, top, total, mixed):
            fade = jnp.exp2(before - top)
            mixed = (mixed + mixed_ref[slot] * fade) * (1.0 / (total + total_ref[slot] * fade))
            rows = pl.ds(pl.multiple_of(step * LANES + parity * HD, HD), HD)
            attn_ref[rows, patch * PATCH : (patch + 1) * PATCH] = mixed.astype(jnp.bfloat16)

        attend([step], patches, True, parts_of, q_ref, k_ref, vt_ref, top_ref, finish)
        rows = pl.ds(pl.multiple_of(step * LANES, LANES), LANES)
        total = jnp.dot(attn_ref[rows, :], cot_ref[...], preferred_element_type=jnp.float32).astype(jnp.bfloat16)
        for part in range(per_pair):
            gsend_ref[step * per_pair + part] = total[part * grain : (part + 1) * grain]
        for part in range(per_pair):
            index = step * per_pair + part

            @pl.when(lax.rem(lax.div(index, per_owner), 2) != core)
            def _():
                pair_copy(index)[1].start()

        @pl.when(turn > 0)
        def _():
            gather_pair(step_of(turn - 1))

        return carry

    lax.fori_loop(0, pairs, pair, 0)
    gather_pair(step_of(pairs - 1))
    mixture = lax.dot_general(
        attn_ref[...], weight_ref[7], (((0,), (0,)), ((), ())), preferred_element_type=jnp.float32
    )
    block_ref[...] = (hid_ref[...].reshape(patches * PATCH, features).astype(jnp.float32) + mixture).astype(jnp.bfloat16)
    write = pltpu.make_async_copy(block_ref, out_ref, load_sem.at[0])
    write.start()
    sums = []
    for part in range(per_owner):
        sums.append(gsum_ref[chip * per_owner + part].astype(jnp.float32))
        for k in range(chips - 1):
            slot = k * per_owner + part
            remote(gsum_ref.at[0], grecv_ref.at[slot], share_send.at[0], share_recv.at[slot],
                   {"space": partner}).wait_recv()
            sums[-1] = sums[-1] + grecv_ref[slot].astype(jnp.float32)
    gathered = jnp.concatenate(sums, axis=0)
    piece = share // levels
    strips = lsend_ref.shape[0]
    width = features // strips
    for strip in range(strips):
        for i in range(levels):
            lsend_ref[strip, i] = gathered[
                i * piece : (i + 1) * piece, strip * width : (strip + 1) * width
            ].astype(jnp.bfloat16)
    parts, fulls = [], []
    for strip in range(strips):
        for k, peer in enumerate(peers):
            parts.append(remote(lsend_ref.at[strip, peer], lrecv_ref.at[strip, k], part_send.at[strip, k],
                                part_recv.at[strip, k], {"level": peer}))
            parts[-1].start()
    for steps in inward + back + [[make() for make in sent]]:
        for step in steps:
            step.wait_send()

    def drained(slot, carry):
        index = lax.div(slot, per_owner) * 2 * per_owner + (1 - core) * per_owner + lax.rem(slot, per_owner)
        pair_copy(index)[1].wait_send()
        owner, copy = share_copy(slot)

        @pl.when(owner != chip)
        def _():
            copy.wait_send()

        return carry

    lax.fori_loop(0, chips * per_owner, drained, 0)

    for strip in range(strips):
        gathered = lsend_ref[strip, level].astype(jnp.float32)
        for k in range(levels - 1):
            parts[strip * (levels - 1) + k].wait_recv()
            gathered = gathered + lrecv_ref[strip, k].astype(jnp.float32)
        final_ref[strip, level] = gathered.astype(jnp.bfloat16)
        for k, peer in enumerate(peers):
            fulls.append(remote(final_ref.at[strip, level], final_ref.at[strip, level], full_send.at[strip, k],
                                full_recv.at[strip, k], {"level": peer}))
            fulls[-1].start()
    for step in fulls:
        step.wait_recv()
    for strip in range(strips):
        for i in range(levels):
            grad_ref[i * piece : (i + 1) * piece, strip * width : (strip + 1) * width] = final_ref[strip, i].astype(
                jnp.float32
            )
    for step in parts + fulls:
        step.wait_send()
    write.wait()


def body(fields, norm_vert, query_vert, keys_vert, values_vert, out_vert, level_bias, norm_patch, query_patch,
         keys_patch, values_patch, out_patch, patch_bias, neighbours, counts, cotangent):
    _, tokens, features = fields.shape
    levels = lax.axis_size("level")
    cycle = lax.axis_size("space")
    patches = tokens // PATCH
    columns = ROWS
    size = levels * columns
    chunks = tokens // size
    pairs = features // LANES
    grain = math.gcd(features // cycle, LANES)
    share = features // cycle
    x = fields.reshape(chunks, levels, columns, features)
    vmem = pl.BlockSpec(memory_space=pltpu.VMEM)
    smem = pl.BlockSpec(memory_space=pltpu.SMEM)
    hbm = pl.BlockSpec(memory_space=pl.ANY)
    narrow = lambda *shape: pltpu.VMEM(shape, jnp.bfloat16)
    dma = lambda *shape: pltpu.SemaphoreType.DMA(shape)
    blocks = 5 * patches
    out, grad = pl.pallas_call(
        functools.partial(whole_kernel, cycle, levels),
        out_shape=(
            jax.ShapeDtypeStruct((tokens, features), jnp.bfloat16),
            jax.ShapeDtypeStruct((share, features), jnp.float32),
        ),
        in_specs=[vmem] * 3 + [hbm] * 9 + [smem] * 4,
        out_specs=(hbm, vmem),
        scratch_shapes=[
            narrow(tokens, features),
            narrow(8, features, features),
            narrow(features, features),
            narrow(features, LANES),
            narrow(LANES, features),
            narrow(tokens, features),
            narrow(chunks, levels, columns, features),
            narrow(chunks, levels, columns, features),
            narrow(chunks, levels, columns, features),
            narrow(chunks, size, features),
            narrow(4, chunks, size, features),
            narrow(tokens, features),
            narrow(blocks, PATCH, features),
            narrow(blocks, features, PATCH),
            narrow(features, tokens),
            narrow(features // grain, grain, features),
            narrow(features // grain // 2, grain, features),
            narrow(features // grain // 2, grain, features),
            narrow((cycle // 2 - 1) * share // grain, grain, features),
            narrow(STRIPS, levels, share // levels, features // STRIPS),
            narrow(STRIPS, levels - 1, share // levels, features // STRIPS),
            narrow(STRIPS, levels, share // levels, features // STRIPS),
            pltpu.VMEM((patches * pairs * 2, 1, PATCH), jnp.float32),
            pltpu.VMEM((patches * pairs * 2, 1, PATCH), jnp.float32),
            pltpu.VMEM((patches * pairs * 2, HD, PATCH), jnp.float32),
            dma(9),
            dma(chunks, levels - 1),
            dma(chunks, levels - 1),
            dma(chunks, levels - 1),
            dma(chunks, levels - 1),
            dma(chunks, 4),
            dma(chunks, 4),
            dma(features // grain // 2),
            dma(features // grain // 2),
            dma(features // grain // 2),
            dma((cycle // 2 - 1) * share // grain),
            dma(STRIPS, levels - 1),
            dma(STRIPS, levels - 1),
            dma(STRIPS, levels - 1),
            dma(STRIPS, levels - 1),
        ],
        compiler_params=pltpu.CompilerParams(
            collective_id=0, has_side_effects=True, vmem_limit_bytes=VMEM_LIMIT
        ),
        name="whole_block",
    )(x, norm_vert, norm_patch, query_vert, keys_vert, values_vert, out_vert, query_patch, keys_patch,
      values_patch, out_patch, cotangent[0], jnp.transpose(level_bias, (1, 2, 0)), patch_bias.T, neighbours, counts)
    return (out[None], grad)


def solution(mesh):
    split = P("level", "space", None)
    return jax.shard_map(
        body,
        mesh=mesh,
        in_specs=(split,) + (P(),) * 12 + (P("space", None), P("space"), split),
        out_specs=(split, P("space", None)),
        check_vma=False,
    )
```
